128 devices in a mesh: pairs: 128 (over z, x, y, core).
Axes of the slice: x: 4, y: 4, z: 4, core: 2. Of those that a mesh axis runs over, the one named last changes fastest.
Arguments:
- pno_basis: bfloat16 [1024, 192, 128], P('pairs'), may hold values from -0.4375 to 0.4375
- pno_count: int32 [1024], P('pairs'), may hold values from 64 to 128
- partner_owner: int32 [1024, 12], P('pairs'), may hold values from 0 to 127, all different within a row; in each aligned block of 8 rows (0 to 7, 8 to 15, ...) at most 2 rows name the same one
- partner_local: int32 [1024, 12], P('pairs'), may hold values from 0 to 7
- exchange_k: bfloat16 [1024, 128, 128], P('pairs'), may hold values from -6 to 6
- ladder_factor: bfloat16 [1024, 40, 128, 128], P('pairs'), may hold values from -0.15625 to 0.15625
- pno_energy: float32 [1024, 128], P('pairs'), may hold values from 0.3 to 3
- occ_energy: float32 [1024], P('pairs'), may hold values from -2 to -0.6
- coupling_fock: bfloat16 [1024, 12], P('pairs'), may hold values from -3 to 3
Outputs:
- amplitudes: float32 [1024, 128, 128], P('pairs')
The draws below stay inside these ranges and needn't reach their ends.
Inputs may be any that keep to these rules, and one draw needn't show every extreme that they name: `partner_owner`: the 12 partners of one pair have different owners. Among the 8 pairs of one device no device is named more than 2 times, and in some devices' pairs one device is named exactly 2 times. Partner c of pair p is the pair numbered partner_owner[p, c] * 8 + partner_local[p, c]. Pair p uses its first pno_count[p] orbitals; the others are padding.
All inputs are finite; a program needn't handle non-finite values.
Results may differ from the reference program's by a relative error of at most 0.009.
Values may be sent and summed in bfloat16 or wider, within the bound.
No kernel may reach another device: no remote copies, remote signals or barrier semaphores. Data moves between devices by JAX's collectives and lax.ppermute only.
A program may use at most 128 MiB of HBM per device.

```python
import math
import jax
import jax.numpy as jnp
import numpy as np
from jax import lax

NPNO = 128
NV = 192
NAUX = 40
NCOUP = 12
ITERS = 3
PAIRS_DEV = 8
PAIRS = 1024
MOST = 2
N_PAIRS = 128


def set_ends(result, stream_key, smallest, top_value):
    extent = result.shape
    spot = [jax.random.randint(jax.random.fold_in(stream_key, axis), (), 0, extent[axis]) for axis in range(len(extent))]
    result = result.at[tuple(spot)].set(smallest)
    longest = extent.index(max(extent))
    spot[longest] = (spot[longest] + 1) % extent[longest]
    return result.at[tuple(spot)].set(top_value)


def block_levels(key, dims, shards, least, high):
    level = 1.0
    for dim, parts in shards:
        draws = jax.random.uniform(jax.random.fold_in(jax.random.fold_in(key, 6), dim), (parts,), jnp.float32, least / len(shards), high / len(shards))
        level = level * jnp.repeat(jnp.exp(draws), dims[dim] // parts).reshape((-1,) + (1,) * (len(dims) - 1 - dim))
    return level


def shared_out(rng, own, number, rows, amount, top, bound, skew):
    sequence = jax.random.permutation(rng, amount)
    packed, common = load_shares(amount, rows * top, bound, skew, True), load_shares(amount, rows * top, bound, skew, False)
    places = jnp.arange(amount)

    def named(sizes, turn):
        used = int((sizes > 0).sum())
        fixed = max(1, used // 4)
        passed = fixed + (places - fixed + turn * (used - fixed)) % max(1, amount - fixed)
        return jnp.zeros((amount,), jnp.int32).at[sequence[jnp.where(places < fixed, places, passed)]].set(jnp.asarray(sizes, jnp.int32))

    sizes = jnp.where(number % 4 == 0, named(packed, number // 4), named(common, number - number // 4 - 1))
    mixed = jax.random.permutation(jax.random.fold_in(own, 3), amount)
    giver, taker = mixed[0:amount // 2 * 2:2], mixed[1:amount // 2 * 2:2]
    room = jnp.minimum(sizes[giver] - 1, bound - sizes[taker]) // 2
    room = jnp.where((giver == sequence[0]) | (taker == sequence[0]) | (sizes[taker] == 0), 0, jnp.maximum(room, 0))
    passed = jax.random.randint(jax.random.fold_in(own, 4), (amount // 2,), 0, 1 << 20) % (room + 1)
    sizes = sizes.at[giver].add(-passed).at[taker].add(passed)
    labels = jnp.searchsorted(jnp.cumsum(sizes), jnp.arange(rows * top), side="right").astype(jnp.int32)
    table = labels.reshape(top, rows).T
    table = table[jax.random.permutation(jax.random.fold_in(own, 1), rows)]
    turn = jax.random.randint(jax.random.fold_in(own, 2), (rows, 1), 0, top)
    return jnp.take_along_axis(table, (jnp.arange(top)[None, :] + turn) % top, axis=1)


def load_shares(count, total, bound, lean, full):
    loads = [(1 << 20) // math.isqrt(grade ** lean) + 1 for grade in range(1, count + 1)]
    largest = bound if full else min(bound, max(-(-total // count), total * loads[0] // sum(loads)))
    least = 1 if total - largest >= count - 1 else 0
    given, rest = [largest] + [least] * (count - 1), total - largest - least * (count - 1)
    while rest > 0:
        candidates = [i for i in range(1, count) if given[i] < largest] or [i for i in range(1, count) if given[i] < bound]
        pool, remaining = sum([loads[i] for i in candidates]), rest
        for i in candidates:
            more = min(bound - given[i], max(1, remaining * loads[i] // pool), rest)
            given[i] = given[i] + more
            rest = rest - more
    return np.array(given)


def centred(own_key, extent, spread, limit, split=(), kind=jnp.bfloat16):
    result = jax.random.normal(own_key, extent, jnp.float32) * spread
    if len(split) > 0:
        result = block_levels(own_key, extent, split, -0.22, 0.18) * result
    return jnp.clip(result, min=-limit, max=limit).astype(kind)


def setup_inputs(seed: int = 0) -> dict:
    arg_keys = jax.random.split(jax.random.key(seed), 10)
    pno_basis = centred(arg_keys[0], (PAIRS, NV, NPNO), NV ** -0.5, 0.4375, ((0, 128),))
    pno_count = set_ends(jax.random.randint(arg_keys[1], (PAIRS,), NPNO // 2, NPNO + 1), jax.random.fold_in(arg_keys[1], 1), NPNO // 2, NPNO).astype(jnp.int32)
    partner_owner_keys = jax.random.split(jax.random.fold_in(arg_keys[2], 1), PAIRS // PAIRS_DEV)
    partner_owner_turns = jax.random.permutation(jax.random.fold_in(arg_keys[2], 3), PAIRS // PAIRS_DEV)
    partner_owner = jax.vmap(lambda own, number: shared_out(jax.random.fold_in(arg_keys[2], 2), own, number, PAIRS_DEV, N_PAIRS, NCOUP, MOST, 2))(partner_owner_keys, partner_owner_turns).reshape((PAIRS, NCOUP))
    partner_local = set_ends(jax.random.randint(arg_keys[3], (PAIRS, NCOUP), 0, PAIRS_DEV), jax.random.fold_in(arg_keys[3], 1), 0, PAIRS_DEV - 1).astype(jnp.int32)
    exchange_k = centred(arg_keys[4], (PAIRS, NPNO, NPNO), 1.0, 6.0, ((0, 128),))
    ladder_factor = centred(arg_keys[5], (PAIRS, NAUX, NPNO, NPNO), (NPNO * NAUX // 4) ** -0.5, 0.15625, ((0, 128),))
    pno_energy = jnp.clip(jnp.exp(math.log(3.0) - 2.3025851 * jax.random.uniform(arg_keys[6], (PAIRS, NPNO), jnp.float32) ** block_levels(arg_keys[6], (PAIRS, NPNO), ((0, 128),), -0.2, 0.2)), 0.3, 3.0)
    occ_energy = jnp.clip(-2.0 + 1.4 * jax.random.uniform(arg_keys[7], (PAIRS,), jnp.float32) ** block_levels(arg_keys[7], (PAIRS,), ((0, 128),), -0.2, 0.2), -2.0, -0.6)
    coupling_fock = centred(arg_keys[8], (PAIRS, NCOUP), 0.5, 3.0, ((0, 128),))
    return {"pno_basis": pno_basis, "pno_count": pno_count, "partner_owner": partner_owner, "partner_local": partner_local, "exchange_k": exchange_k, "ladder_factor": ladder_factor, "pno_energy": pno_energy, "occ_energy": occ_energy, "coupling_fock": coupling_fock}


level_shift = 0.3


def reference(pno_basis, pno_count, partner_owner, partner_local, exchange_k, ladder_factor, pno_energy, occ_energy, coupling_fock):
    columns = lax.broadcasted_iota(jnp.int32, (PAIRS, NPNO), 1)
    live_cols = (columns < pno_count[:, None]).astype(jnp.float32)
    masked_basis = (pno_basis.astype(jnp.float32) * live_cols[:, None, :]).astype(jnp.bfloat16)
    partner_ids = (partner_owner * PAIRS_DEV + partner_local).astype(jnp.int32)
    block_count = PAIRS // PAIRS_DEV
    block_numbers = jnp.arange(block_count, dtype=jnp.int32)

    def margin_block(block_index):
        first_row = (block_index * PAIRS_DEV).astype(jnp.int32)
        own_basis = lax.dynamic_slice_in_dim(masked_basis, first_row, PAIRS_DEV, 0).astype(jnp.float32)
        chosen = lax.dynamic_slice_in_dim(partner_ids, first_row, PAIRS_DEV, 0)
        other_basis = masked_basis[chosen].astype(jnp.float32)
        product = jnp.einsum("rva,rcvb->rcab", own_basis, other_basis, precision=lax.Precision.HIGHEST)
        return product.astype(jnp.bfloat16)

    margin = lax.map(margin_block, block_numbers).reshape(PAIRS, NCOUP, NPNO, NPNO)
    energy_sum = pno_energy[:, :, None] + pno_energy[:, None, :] - occ_energy[:, None, None]
    divisor = energy_sum + level_shift
    driving = exchange_k.astype(jnp.float32) * (live_cols[:, :, None] * live_cols[:, None, :])
    amplitudes = -driving / divisor
    weights = coupling_fock.astype(jnp.float32)
    for iteration in range(ITERS):
        sent_amps = amplitudes.astype(jnp.bfloat16)

        def couple_block(block_index):
            first_row = (block_index * PAIRS_DEV).astype(jnp.int32)
            block_margin = lax.dynamic_slice_in_dim(margin, first_row, PAIRS_DEV, 0).astype(jnp.float32)
            chosen = lax.dynamic_slice_in_dim(partner_ids, first_row, PAIRS_DEV, 0)
            block_weights = lax.dynamic_slice_in_dim(weights, first_row, PAIRS_DEV, 0)
            partner_amps = sent_amps[chosen].astype(jnp.float32)
            left_half = jnp.einsum("rcab,rcbd->rcad", block_margin, partner_amps, precision=lax.Precision.HIGHEST)
            left_half = left_half * block_weights[:, :, None, None]
            left_half = lax.optimization_barrier(left_half.astype(jnp.bfloat16)).astype(jnp.float32)
            coupling_terms = jnp.einsum("rcad,rced->rcae", left_half, block_margin, precision=lax.Precision.HIGHEST)
            coupling_terms = lax.optimization_barrier(coupling_terms.astype(jnp.bfloat16)).astype(jnp.float32)
            own_amps = lax.dynamic_slice_in_dim(sent_amps, first_row, PAIRS_DEV, 0).astype(jnp.float32)
            factors = lax.dynamic_slice_in_dim(ladder_factor, first_row, PAIRS_DEV, 0).astype(jnp.float32)
            ladder_half = jnp.einsum("rqac,rcd->rqad", factors, own_amps, precision=lax.Precision.HIGHEST)
            ladder_half = lax.optimization_barrier(ladder_half.astype(jnp.bfloat16)).astype(jnp.float32)
            ladder = jnp.einsum("rqad,rqbd->rab", ladder_half, factors, precision=lax.Precision.HIGHEST)
            return jnp.sum(coupling_terms, axis=1) + ladder

        coupled = lax.map(couple_block, block_numbers).reshape(PAIRS, NPNO, NPNO)
        residual = driving + energy_sum * amplitudes + coupled
        amplitudes = amplitudes - residual / divisor
    return amplitudes
```

```python
import functools

import jax
import jax.numpy as jnp
from jax import lax
from jax.experimental import pallas as pl
from jax.experimental.pallas import tpu as pltpu
from jax.sharding import PartitionSpec as P

ITERS = 3
LEVEL_SHIFT = 0.3
LANES = 128
F32 = jnp.float32
BF16 = jnp.bfloat16
NT = (((1,), (1,)), ((), ()))


def regroup(major, minor, turned):
    size = major * minor
    row = lax.broadcasted_iota(jnp.int32, (size, size), 0)
    col = lax.broadcasted_iota(jnp.int32, (size, size), 1)
    to, source = (col, row) if turned else (row, col)
    hit = source == lax.rem(to, major) * minor + lax.div(to, major)
    return jnp.where(hit, 1.0, 0.0).astype(BF16)


def side_by_side(matrix, chips):
    parts = matrix.shape[0] // chips
    return jnp.concatenate([matrix[i * chips : (i + 1) * chips] for i in range(parts)], axis=1)


def one_below_other(pieces):
    parts = pieces.shape[1] // LANES
    return jnp.concatenate([pieces[:, i * LANES : (i + 1) * LANES] for i in range(parts)], axis=0)


def store_pieces(stacked, send_ref, first_lane):
    chips, _, own, _ = send_ref.shape
    width = stacked.shape[1]
    back = regroup(chips, own, True)
    pieces = jnp.dot(back, stacked, preferred_element_type=F32).astype(BF16)
    pieces = pieces.reshape(chips, own, width)
    for core in range(2):
        send_ref[:, core, :, first_lane : first_lane + width] = pieces


def pack_kernel(sent_ref, basis_ref, asked_ref, send_ref):
    chips, _, own, width = send_ref.shape
    stacked = jnp.concatenate(
        [
            jnp.concatenate(
                [side_by_side(sent_ref[p], chips), side_by_side(basis_ref[p], chips)], axis=1
            )
            for p in range(own)
        ],
        axis=0,
    )
    store_pieces(stacked, send_ref, 0)
    send_ref[:, :, :, width - LANES :] = jnp.broadcast_to(
        asked_ref[...][None], (chips, 2, own, LANES)
    )


def pack(sent, masked_basis, asked, chips):
    own = sent.shape[0]
    width = (sent.shape[1] + masked_basis.shape[1]) // chips * LANES + LANES
    return pl.pallas_call(
        pack_kernel,
        out_shape=jax.ShapeDtypeStruct((chips, 2, own, width), BF16),
        name="pack",
    )(sent, masked_basis, asked)


def pick_kernel(list_ref, table_ref, out_ref, onehot_ref):
    half, group = list_ref.shape[1:]
    rows = table_ref.shape[0]
    lane = lax.broadcasted_iota(jnp.int32, (half, LANES), 1)
    for member in range(group):
        wanted = jnp.broadcast_to(list_ref[0, :, member : member + 1], (half, LANES))
        for tile in range(rows // LANES):
            hit = (wanted - tile * LANES) == lane
            onehot_ref[member * half : (member + 1) * half, tile * LANES : (tile + 1) * LANES] = (
                jnp.where(hit, 1.0, 0.0).astype(BF16)
            )
    picked = jnp.dot(onehot_ref[...], table_ref[...], preferred_element_type=F32)
    out_ref[...] = picked.astype(BF16).reshape(out_ref.shape)


def pick_pieces(lists, table, width):
    groups, half, group = lists.shape
    rows = table.shape[0]
    return pl.pallas_call(
        pick_kernel,
        grid=(groups,),
        in_specs=[
            pl.BlockSpec((1, half, group), lambda g: (g, 0, 0)),
            pl.BlockSpec((rows, width), lambda g: (0, 0)),
        ],
        out_specs=pl.BlockSpec((group, half, width), lambda g: (g, 0, 0)),
        out_shape=jax.ShapeDtypeStruct((groups * group, half, width), BF16),
        scratch_shapes=[pltpu.VMEM((group * half, rows), BF16)],
        cost_estimate=pl.CostEstimate(
            flops=2 * groups * group * half * rows * width,
            bytes_accessed=2 * (rows * width + groups * group * half * width),
            transcendentals=0,
        ),
        name="pick_pieces",
    )(lists, table)


def couple_kernel(first, last, *refs):
    refs = list(refs)
    weight_ref, arrived_ref = refs.pop(0), refs.pop(0)
    margin_in = refs.pop(0)
    amp_ref, rest_ref, div_ref = refs.pop(0), refs.pop(0), refs.pop(0)
    out_ref = refs.pop(0)
    sent_ref = send_ref = margin_out = None
    if not last:
        sent_ref, send_ref = refs.pop(0), refs.pop(0)
    if first:
        margin_out = refs.pop(0)
    total_ref, order_ref = refs
    step, steps = pl.program_id(0), pl.num_programs(0)
    chips, _, _, own, width = arrived_ref.shape

    @pl.when(step == 0)
    def _():
        total_ref[...] = jnp.zeros_like(total_ref)
        order_ref[...] = regroup(chips, own, False)

    for core in range(2):
        arrived = arrived_ref[:, core, 0].reshape(chips * own, width)
        ordered = jnp.dot(order_ref[...], arrived, preferred_element_type=F32).astype(BF16)
        for p in range(own):
            pieces = ordered[p * chips : (p + 1) * chips]
            amps = one_below_other(pieces[:, : 2 * LANES])
            if first:
                basis = one_below_other(pieces[:, 2 * LANES :])
                margin = jnp.dot(margin_in[p], basis, preferred_element_type=F32).astype(BF16)
                margin_out[0, core, p] = margin
            else:
                margin = margin_in[0, core, p]
            left = jnp.dot(margin, amps, preferred_element_type=F32)
            left = (left * weight_ref[p, core * steps + step]).astype(BF16)
            term = lax.dot_general(left, margin, NT, preferred_element_type=F32)
            total_ref[p] += term.astype(BF16).astype(F32)

    @pl.when(step == steps - 1)
    def _():
        for p in range(own):
            out_ref[p] = amp_ref[p] - (rest_ref[p] + total_ref[p]) / div_ref[p]
        if not last:
            sent_ref[...] = out_ref[...].astype(BF16)
            stacked = jnp.concatenate(
                [side_by_side(sent_ref[p], chips) for p in range(own)], axis=0
            )
            store_pieces(stacked, send_ref, 0)


def couple(first, last, weights, arrived, margin, amplitudes, rest, divisor):
    chips, _, steps, own, width = arrived.shape
    orbitals = amplitudes.shape[1]
    whole = pl.BlockSpec(amplitudes.shape, lambda c: (0, 0, 0))
    margin_spec = pl.BlockSpec((1, 2, own, orbitals, orbitals), lambda c: (c, 0, 0, 0, 0))
    margin_shape = jax.ShapeDtypeStruct((steps, 2, own, orbitals, orbitals), BF16)
    out_specs, out_shape = [whole], [jax.ShapeDtypeStruct(amplitudes.shape, F32)]
    if not last:
        send = (chips, 2, own, 2 * LANES)
        out_specs += [whole, pl.BlockSpec(send, lambda c: (0, 0, 0, 0))]
        out_shape += [
            jax.ShapeDtypeStruct(amplitudes.shape, BF16),
            jax.ShapeDtypeStruct(send, BF16),
        ]
    if first:
        out_specs.append(margin_spec)
        out_shape.append(margin_shape)
    return pl.pallas_call(
        functools.partial(couple_kernel, first, last),
        grid=(steps,),
        in_specs=[
            pl.BlockSpec(memory_space=pltpu.SMEM),
            pl.BlockSpec((chips, 2, 1, own, width), lambda c: (0, 0, c, 0, 0)),
            pl.BlockSpec(margin.shape, lambda c: (0, 0, 0)) if first else margin_spec,
            whole,
            whole,
            whole,
        ],
        out_specs=out_specs,
        out_shape=out_shape,
        scratch_shapes=[
            pltpu.VMEM(amplitudes.shape, F32),
            pltpu.VMEM((own * chips, own * chips), BF16),
        ],
        name="couple",
    )(weights, arrived, margin, amplitudes, rest, divisor)


def swap(values):
    return lax.all_to_all(values, "pairs", split_axis=0, concat_axis=0, tiled=True)


def shards(
    pno_basis,
    pno_count,
    partner_owner,
    partner_local,
    exchange_k,
    ladder_factor,
    pno_energy,
    occ_energy,
    coupling_fock,
):
    devices = lax.axis_size("pairs")
    chips = devices // 2
    own, domain, orbitals = pno_basis.shape
    fitted = ladder_factor.shape[1]
    partners = partner_owner.shape[1]
    half = own * partners // 2
    rows = devices * own
    group = 16
    columns = lax.broadcasted_iota(jnp.int32, (own, orbitals), 1)
    live_cols = (columns < pno_count[:, None]).astype(F32)
    masked_basis = pno_basis * live_cols[:, None, :].astype(BF16)
    energy_sum = pno_energy[:, :, None] + pno_energy[:, None, :] - occ_energy[:, None, None]
    divisor = energy_sum + LEVEL_SHIFT
    driving = exchange_k.astype(F32) * (live_cols[:, :, None] * live_cols[:, None, :])
    amplitudes = -driving / divisor
    weights = coupling_fock.astype(F32)

    asked = jnp.stack([partner_owner, partner_local], axis=0).astype(BF16)
    asked = asked.reshape(2, own, 2, partners // 2)
    asked = jnp.transpose(asked, (2, 0, 3, 1)).reshape(2, 2, half)
    asked = jnp.pad(asked, ((0, 0), (0, own - 2), (0, LANES - half)))

    def ladder_of(sent):
        group_width = 8

        def add_group(group_index, total):
            factors = lax.dynamic_slice_in_dim(
                ladder_factor, group_index * group_width, group_width, 1
            )
            ladder_half = jnp.einsum(
                "rqac,rcd->rqad", factors, sent, preferred_element_type=F32
            ).astype(BF16)
            return total + jnp.einsum(
                "rqad,rqbd->rab", ladder_half, factors, preferred_element_type=F32
            )

        return lax.fori_loop(
            0, fitted // group_width, add_group, jnp.zeros((own, orbitals, orbitals), F32)
        )

    sent = amplitudes.astype(BF16)
    send = pack(sent, masked_basis, asked, chips)
    margin = jnp.transpose(masked_basis, (0, 2, 1))
    lists = None
    for iteration in range(ITERS):
        first, last = iteration == 0, iteration == ITERS - 1
        held = swap(send.reshape(devices, own, send.shape[-1]))
        width = 2 * LANES
        if first:
            width = held.shape[-1] - LANES
            names = held[:, :2, width : width + half].astype(jnp.int32)
            lists = names[:, 0] * own + names[:, 1]
            lists = jnp.transpose(lists.reshape(devices // group, group, half), (0, 2, 1))
        arrived = swap(pick_pieces(lists, held.reshape(rows, held.shape[-1]), width))
        rest = driving + energy_sum * amplitudes + ladder_of(sent)
        results = couple(
            first,
            last,
            weights,
            arrived.reshape(chips, 2, partners // 2, own, width),
            margin,
            amplitudes,
            rest,
            divisor,
        )
        amplitudes = results[0]
        if not last:
            sent, send = results[1], results[2]
        if first:
            margin = results[3]
    return amplitudes


def solution(mesh):
    return jax.shard_map(
        shards,
        mesh=mesh,
        in_specs=(
            P("pairs", None, None),
            P("pairs"),
            P("pairs", None),
            P("pairs", None),
            P("pairs", None, None),
            P("pairs", None, None, None),
            P("pairs", None),
            P("pairs"),
            P("pairs", None),
        ),
        out_specs=P("pairs", None, None),
        check_vma=False,
    )
```

```python
import functools

import jax
import jax.numpy as jnp
from jax import lax
from jax.experimental import pallas as pl
from jax.experimental.pallas import tpu as pltpu
from jax.sharding import PartitionSpec as P

ITERS = 3
LEVEL_SHIFT = 0.3
LANES = 128
TURN = 32
F32 = jnp.float32
BF16 = jnp.bfloat16
NT = (((1,), (1,)), ((), ()))


def regroup(major, minor, turned):
    size = major * minor
    row = lax.broadcasted_iota(jnp.int32, (size, size), 0)
    col = lax.broadcasted_iota(jnp.int32, (size, size), 1)
    to, source = (col, row) if turned else (row, col)
    hit = source == lax.rem(to, major) * minor + lax.div(to, major)
    return jnp.where(hit, 1.0, 0.0).astype(BF16)


def part(values, index):
    return values[:, index * LANES : (index + 1) * LANES]


def store_pieces(stack, send_ref, first_lane):
    chips, _, own, _ = send_ref.shape
    parts = stack[0].shape[0] // chips
    back = regroup(TURN, own, True)
    for start in range(0, chips, TURN):
        rows = jnp.concatenate(
            [
                jnp.concatenate(
                    [m[i * chips + start : i * chips + start + TURN] for i in range(parts)], axis=1
                )
                for m in stack
            ],
            axis=0,
        )
        pieces = jnp.dot(back, rows, preferred_element_type=F32).astype(BF16)
        pieces = pieces.reshape(TURN, own, parts * LANES)
        for core in range(2):
            send_ref[start : start + TURN, core, :, first_lane : first_lane + parts * LANES] = (
                pieces
            )


def start_kernel(
    count_ref, occ_ref, owner_ref, local_ref, basis_ref, exchange_ref, energy_ref,
    amp_ref, sent_ref, turned_ref, send_ref,
):
    chips, _, own, width = send_ref.shape
    domain, orbitals = basis_ref.shape[1:]
    row = lax.broadcasted_iota(jnp.int32, (orbitals, orbitals), 0)
    col = lax.broadcasted_iota(jnp.int32, (orbitals, orbitals), 1)
    basis_col = lax.broadcasted_iota(jnp.int32, (domain, orbitals), 1)
    stack = []
    for p in range(own):
        count = count_ref[p]
        live = jnp.logical_and(row < count, col < count)
        energy = jnp.broadcast_to(energy_ref[p : p + 1, :], (orbitals, orbitals))
        energy_sum = energy.T + energy - occ_ref[p]
        driving = jnp.where(live, exchange_ref[p].astype(F32), 0.0)
        amplitudes = -driving / (energy_sum + LEVEL_SHIFT)
        amp_ref[p] = amplitudes
        sent = amplitudes.astype(BF16)
        sent_ref[p] = sent
        masked = jnp.where(basis_col < count, basis_ref[p].astype(F32), 0.0)
        turned_ref[p] = masked.T.astype(BF16)
        stack.append(jnp.concatenate([sent, masked.astype(BF16)], axis=0))
    store_pieces(stack, send_ref, 0)
    half = owner_ref.shape[1] // 2
    empty = jnp.zeros((own, LANES - 2 * half), F32)
    for core in range(2):
        mine = slice(core * half, (core + 1) * half)
        asked = jnp.concatenate(
            [owner_ref[:, mine].astype(F32), local_ref[:, mine].astype(F32), empty], axis=1
        )
        send_ref[:, core, :, width - LANES :] = jnp.broadcast_to(
            asked.astype(BF16)[None], (chips, own, LANES)
        )


def start(count, occ, owner, local, basis, exchange, energy, chips):
    own, domain, orbitals = basis.shape
    width = ((orbitals + domain) // chips + 1) * LANES
    scalars, vectors = pl.BlockSpec(memory_space=pltpu.SMEM), pl.BlockSpec(memory_space=pltpu.VMEM)
    return pl.pallas_call(
        start_kernel,
        in_specs=[scalars] * 2 + [vectors] * 5,
        out_specs=[vectors] * 4,
        out_shape=[
            jax.ShapeDtypeStruct((own, orbitals, orbitals), F32),
            jax.ShapeDtypeStruct((own, orbitals, orbitals), BF16),
            jax.ShapeDtypeStruct((own, orbitals, domain), BF16),
            jax.ShapeDtypeStruct((chips, 2, own, width), BF16),
        ],
        name="start",
    )(count, occ, owner, local, basis, exchange, energy)


def pick_kernel(list_ref, table_ref, out_ref, onehot_ref):
    half, group = list_ref.shape[1:]
    rows, width = table_ref.shape
    lane = lax.broadcasted_iota(jnp.int32, (half, LANES), 1).astype(F32).astype(BF16)
    one, zero = jnp.bfloat16(1), jnp.bfloat16(0)
    at_once = 4
    for begin in range(0, group, at_once):
        for member in range(begin, begin + at_once):
            wanted = jnp.broadcast_to(list_ref[0, :, member : member + 1], (half, LANES))
            tile_of = lax.shift_right_logical(wanted, 7).astype(F32).astype(BF16)
            lane_of = jnp.bitwise_and(wanted, LANES - 1).astype(F32).astype(BF16)
            hit = jnp.where(lane_of == lane, one, zero)
            for tile in range(rows // LANES):
                onehot_ref[
                    member * half : (member + 1) * half, tile * LANES : (tile + 1) * LANES
                ] = jnp.where(tile_of == jnp.bfloat16(tile), hit, zero)
        picked = jnp.dot(
            onehot_ref[begin * half : (begin + at_once) * half],
            table_ref[...],
            preferred_element_type=F32,
        )
        out_ref[begin : begin + at_once] = picked.astype(BF16).reshape(at_once, half, width)


def pick_pieces(lists, table, width):
    groups, half, group = lists.shape
    rows = table.shape[0]
    return pl.pallas_call(
        pick_kernel,
        grid=(groups,),
        in_specs=[
            pl.BlockSpec((1, half, group), lambda g: (g, 0, 0)),
            pl.BlockSpec((rows, width), lambda g: (0, 0)),
        ],
        out_specs=pl.BlockSpec((group, half, width), lambda g: (g, 0, 0)),
        out_shape=jax.ShapeDtypeStruct((groups * group, half, width), BF16),
        scratch_shapes=[pltpu.VMEM((group * half, rows), BF16)],
        cost_estimate=pl.CostEstimate(
            flops=2 * groups * group * half * rows * width,
            bytes_accessed=2 * (rows * width + groups * group * half * width),
            transcendentals=0,
        ),
        name="pick_pieces",
    )(lists, table)


def couple_kernel(first, last, *refs):
    refs = list(refs)
    weight_ref, arrived_hbm, margin_hbm = refs[:3]
    amp_hbm, rest_hbm, div_hbm, out_ref = refs[3:7]
    refs = refs[7:]
    if not last:
        sent_ref, send_ref = refs[:2]
        refs = refs[2:]
    if first:
        margin_ref, refs = refs[0], refs[1:]
    other_ref, left_ref, held_ref, amp_ref, rest_ref, div_ref, sems = refs[:7]
    if first:
        turned_ref, basis_ref, arrived_ref = held_ref, refs[7], refs[8]
    else:
        margin_ref, arrived_ref = held_ref, arrived_hbm
    chips, _, steps, own, width = arrived_ref.shape
    orbitals = amp_ref.shape[1]
    blocks = chips // TURN
    copies = []
    if first:
        for i in range(blocks):
            rows = pl.ds(i * TURN, TURN)
            copies.append(
                pltpu.make_async_copy(arrived_hbm.at[rows], arrived_ref.at[rows], sems.at[i])
            )
    for i, (source, target) in enumerate(
        [(margin_hbm, held_ref), (amp_hbm, amp_ref), (rest_hbm, rest_ref), (div_hbm, div_ref)]
    ):
        copies.append(pltpu.make_async_copy(source, target, sems.at[blocks + i]))
    landed = copies[:-4]
    copies = copies[-4:]
    for copy in landed + copies:
        copy.start()
    order = regroup(TURN, own, False)
    for block in range(blocks):
        begin = block * TURN
        if first:
            landed[block].wait()
        for step in range(steps):
            for core in range(2):
                c = core * steps + step
                arrived = arrived_ref[begin : begin + TURN, core, step].reshape(TURN * own, width)
                moved = jnp.dot(order, arrived, preferred_element_type=F32).astype(BF16)
                for p in range(own):
                    rows = moved[p * TURN : (p + 1) * TURN]
                    for i in range(orbitals // chips):
                        place = i * chips + begin
                        other_ref[p, c, place : place + TURN, :] = part(rows, i)
                    for i in range(orbitals // chips, width // LANES):
                        place = i * chips + begin - orbitals
                        basis_ref[p, place : place + TURN, c * LANES : (c + 1) * LANES] = part(
                            rows, i
                        )
    copies[0].wait()
    for p in range(own):
        if first:
            margin_ref[p] = jnp.dot(
                turned_ref[p], basis_ref[p], preferred_element_type=F32
            ).astype(BF16)
        for c in range(2 * steps):
            left = jnp.dot(
                margin_ref[p, :, c * orbitals : (c + 1) * orbitals],
                other_ref[p, c],
                preferred_element_type=F32,
            )
            left_ref[p, :, c * orbitals : (c + 1) * orbitals] = (left * weight_ref[p, c]).astype(
                BF16
            )
    for copy in copies[1:]:
        copy.wait()
    stack = []
    for p in range(own):
        coupled = lax.dot_general(left_ref[p], margin_ref[p], NT, preferred_element_type=F32)
        amplitudes = amp_ref[p] - (rest_ref[p] + coupled) / div_ref[p]
        out_ref[p] = amplitudes
        if not last:
            sent = amplitudes.astype(BF16)
            sent_ref[p] = sent
            stack.append(sent)
    if not last:
        store_pieces(stack, send_ref, 0)


def couple(first, last, weights, arrived, margin, amplitudes, rest, divisor):
    chips, _, steps, own, width = arrived.shape
    orbitals = amplitudes.shape[1]
    vectors = pl.BlockSpec(memory_space=pltpu.VMEM)
    far = pl.BlockSpec(memory_space=pltpu.HBM)
    all_columns = 2 * steps * orbitals
    out_shape = [jax.ShapeDtypeStruct(amplitudes.shape, F32)]
    scratch_shapes = [
        pltpu.VMEM((own, 2 * steps, orbitals, orbitals), BF16),
        pltpu.VMEM((own, orbitals, all_columns), BF16),
        pltpu.VMEM(margin.shape, BF16),
        pltpu.VMEM(amplitudes.shape, F32),
        pltpu.VMEM(amplitudes.shape, F32),
        pltpu.VMEM(amplitudes.shape, F32),
        pltpu.SemaphoreType.DMA((chips // TURN + 4,)),
    ]
    if not last:
        out_shape += [
            jax.ShapeDtypeStruct(amplitudes.shape, BF16),
            jax.ShapeDtypeStruct((chips, 2, own, orbitals // chips * LANES), BF16),
        ]
    if first:
        out_shape.append(jax.ShapeDtypeStruct((own, orbitals, all_columns), BF16))
        scratch_shapes.append(pltpu.VMEM((own, margin.shape[2], all_columns), BF16))
        scratch_shapes.append(pltpu.VMEM(arrived.shape, BF16))
    return pl.pallas_call(
        functools.partial(couple_kernel, first, last),
        in_specs=[pl.BlockSpec(memory_space=pltpu.SMEM), far if first else vectors] + [far] * 4,
        out_specs=[vectors] * len(out_shape),
        out_shape=out_shape,
        scratch_shapes=scratch_shapes,
        compiler_params=None if first else pltpu.CompilerParams(vmem_limit_bytes=48 << 20),
        name="couple",
    )(weights, arrived, margin, amplitudes, rest, divisor)


def swap(values):
    return lax.all_to_all(values, "pairs", split_axis=0, concat_axis=0, tiled=True)


def shards(
    pno_basis,
    pno_count,
    partner_owner,
    partner_local,
    exchange_k,
    ladder_factor,
    pno_energy,
    occ_energy,
    coupling_fock,
):
    devices = lax.axis_size("pairs")
    chips = devices // 2
    own, domain, orbitals = pno_basis.shape
    fitted = ladder_factor.shape[1]
    partners = partner_owner.shape[1]
    half = own * partners // 2
    rows = devices * own
    group = 32
    columns = lax.broadcasted_iota(jnp.int32, (own, orbitals), 1)
    live_cols = (columns < pno_count[:, None]).astype(F32)
    energy_sum = pno_energy[:, :, None] + pno_energy[:, None, :] - occ_energy[:, None, None]
    divisor = energy_sum + LEVEL_SHIFT
    driving = exchange_k.astype(F32) * (live_cols[:, :, None] * live_cols[:, None, :])
    weights = coupling_fock.astype(F32)

    def ladder_of(sent):
        group_width = 8

        def add_group(group_index, total):
            factors = lax.dynamic_slice_in_dim(
                ladder_factor, group_index * group_width, group_width, 1
            )
            ladder_half = jnp.einsum(
                "rqac,rcd->rqad", factors, sent, preferred_element_type=F32
            ).astype(BF16)
            return total + jnp.einsum(
                "rqad,rqbd->rab", ladder_half, factors, preferred_element_type=F32
            )

        return lax.fori_loop(
            0, fitted // group_width, add_group, jnp.zeros((own, orbitals, orbitals), F32)
        )

    amplitudes, sent, margin, send = start(
        pno_count, occ_energy, partner_owner, partner_local, pno_basis, exchange_k, pno_energy, chips
    )
    lists = None
    for iteration in range(ITERS):
        first, last = iteration == 0, iteration == ITERS - 1
        held = swap(send.reshape(devices, own, send.shape[-1]))
        width = 2 * LANES
        if first:
            width = held.shape[-1] - LANES
            names = held[:, :, width : width + partners].astype(jnp.int32)
            lists = names[:, :, : partners // 2] * own + names[:, :, partners // 2 :]
            lists = lists.reshape(devices // group, group, own, partners // 2)
            lists = jnp.transpose(lists, (0, 3, 2, 1)).reshape(devices // group, half, group)
        arrived = swap(pick_pieces(lists, held.reshape(rows, held.shape[-1]), width))
        rest = driving + energy_sum * amplitudes + ladder_of(sent)
        results = couple(
            first,
            last,
            weights,
            arrived.reshape(chips, 2, partners // 2, own, width),
            margin,
            amplitudes,
            rest,
            divisor,
        )
        amplitudes = results[0]
        if not last:
            sent, send = results[1], results[2]
        if first:
            margin = results[3]
    return amplitudes


def solution(mesh):
    return jax.shard_map(
        shards,
        mesh=mesh,
        in_specs=(
            P("pairs", None, None),
            P("pairs"),
            P("pairs", None),
            P("pairs", None),
            P("pairs", None, None),
            P("pairs", None, None, None),
            P("pairs", None),
            P("pairs"),
            P("pairs", None),
        ),
        out_specs=P("pairs", None, None),
        check_vma=False,
    )
```

```python
import functools

import jax
import jax.numpy as jnp
from jax import lax
from jax.experimental import pallas as pl
from jax.experimental.pallas import tpu as pltpu
from jax.sharding import PartitionSpec as P

ITERS = 3
LEVEL_SHIFT = 0.3
LANES = 128
TURN = 32
COUPLE_VMEM = 48 << 20
F32 = jnp.float32
BF16 = jnp.bfloat16
NT = (((1,), (1,)), ((), ()))


def regroup(major, minor, turned):
    size = major * minor
    row = lax.broadcasted_iota(jnp.int32, (size, size), 0)
    col = lax.broadcasted_iota(jnp.int32, (size, size), 1)
    to, source = (col, row) if turned else (row, col)
    hit = source == lax.rem(to, major) * minor + lax.div(to, major)
    return jnp.where(hit, 1.0, 0.0).astype(BF16)


def part(values, index):
    return values[:, index * LANES : (index + 1) * LANES]


def store_pieces(stack, send_ref, first_lane):
    chips, own, _ = send_ref.shape
    parts = stack[0].shape[0] // chips
    back = regroup(TURN, own, True)
    for start in range(0, chips, TURN):
        rows = jnp.concatenate(
            [
                jnp.concatenate(
                    [m[i * chips + start : i * chips + start + TURN] for i in range(parts)], axis=1
                )
                for m in stack
            ],
            axis=0,
        )
        pieces = jnp.dot(back, rows, preferred_element_type=F32).astype(BF16)
        pieces = pieces.reshape(TURN, own, parts * LANES)
        send_ref[start : start + TURN, :, first_lane : first_lane + parts * LANES] = pieces


def start_kernel(
    count_ref, occ_ref, owner_ref, local_ref, basis_ref, exchange_ref, energy_ref,
    amp_ref, sent_ref, turned_ref, send_ref,
):
    chips, own, width = send_ref.shape
    domain, orbitals = basis_ref.shape[1:]
    row = lax.broadcasted_iota(jnp.int32, (orbitals, orbitals), 0)
    col = lax.broadcasted_iota(jnp.int32, (orbitals, orbitals), 1)
    basis_col = lax.broadcasted_iota(jnp.int32, (domain, orbitals), 1)
    stack = []
    for p in range(own):
        count = count_ref[p]
        live = jnp.logical_and(row < count, col < count)
        energy = jnp.broadcast_to(energy_ref[p : p + 1, :], (orbitals, orbitals))
        energy_sum = energy.T + energy - occ_ref[p]
        driving = jnp.where(live, exchange_ref[p].astype(F32), 0.0)
        amplitudes = -driving / (energy_sum + LEVEL_SHIFT)
        amp_ref[p] = amplitudes
        sent = amplitudes.astype(BF16)
        sent_ref[p] = sent
        masked = jnp.where(basis_col < count, basis_ref[p].astype(F32), 0.0)
        turned_ref[p] = masked.T.astype(BF16)
        stack.append(jnp.concatenate([sent, masked.astype(BF16)], axis=0))
    store_pieces(stack, send_ref, 0)
    partners = owner_ref.shape[1]
    empty = jnp.zeros((own, LANES - 2 * partners), F32)
    asked = jnp.concatenate(
        [owner_ref[...].astype(F32), local_ref[...].astype(F32), empty], axis=1
    )
    send_ref[:, :, width - LANES :] = jnp.broadcast_to(
        asked.astype(BF16)[None], (chips, own, LANES)
    )


def start(count, occ, owner, local, basis, exchange, energy, chips):
    own, domain, orbitals = basis.shape
    width = ((orbitals + domain) // chips + 1) * LANES
    scalars, vectors = pl.BlockSpec(memory_space=pltpu.SMEM), pl.BlockSpec(memory_space=pltpu.VMEM)
    return pl.pallas_call(
        start_kernel,
        in_specs=[scalars] * 2 + [vectors] * 5,
        out_specs=[vectors] * 4,
        out_shape=[
            jax.ShapeDtypeStruct((own, orbitals, orbitals), F32),
            jax.ShapeDtypeStruct((own, orbitals, orbitals), BF16),
            jax.ShapeDtypeStruct((own, orbitals, domain), BF16),
            jax.ShapeDtypeStruct((chips, own, width), BF16),
        ],
        name="start",
    )(count, occ, owner, local, basis, exchange, energy)


def pick_kernel(core_ref, list_ref, near_ref, mate_ref, out_ref, onehot_ref):
    half, group = list_ref.shape[1:]
    held, width = near_ref.shape
    lane = lax.broadcasted_iota(jnp.int32, (half, LANES), 1).astype(F32).astype(BF16)
    one, zero = jnp.bfloat16(1), jnp.bfloat16(0)
    at_once = 4
    for begin in range(0, group, at_once):
        for member in range(begin, begin + at_once):
            wanted = jnp.broadcast_to(list_ref[0, :, member : member + 1], (half, LANES))
            tile_of = lax.shift_right_logical(wanted, 7).astype(F32).astype(BF16)
            lane_of = jnp.bitwise_and(wanted, LANES - 1).astype(F32).astype(BF16)
            hit = jnp.where(lane_of == lane, one, zero)
            for tile in range(2 * held // LANES):
                onehot_ref[
                    member * half : (member + 1) * half, tile * LANES : (tile + 1) * LANES
                ] = jnp.where(tile_of == jnp.bfloat16(tile), hit, zero)
        rows = slice(begin * half, (begin + at_once) * half)
        picked = jnp.dot(
            onehot_ref[rows, :held], near_ref[...], preferred_element_type=F32
        ) + jnp.dot(onehot_ref[rows, held:], mate_ref[...], preferred_element_type=F32)
        out_ref[begin : begin + at_once, 0] = picked.astype(BF16).reshape(at_once, half, width)


def pick_pieces(core, lists, near, mate, width):
    groups, half, group = lists.shape
    held = near.shape[0]
    chips = groups * group // 2
    halves = groups // 2
    table = pl.BlockSpec((held, width), lambda g, core: (0, 0))
    return pl.pallas_call(
        pick_kernel,
        grid_spec=pltpu.PrefetchScalarGridSpec(
            num_scalar_prefetch=1,
            grid=(groups,),
            in_specs=[pl.BlockSpec((1, half, group), lambda g, core: (g, 0, 0)), table, table],
            out_specs=pl.BlockSpec(
                (group, 1, half, width),
                lambda g, core: (
                    lax.rem(g, halves),
                    jnp.bitwise_xor(lax.div(g, halves), core[0]),
                    0,
                    0,
                ),
            ),
            scratch_shapes=[pltpu.VMEM((group * half, 2 * held), BF16)],
        ),
        out_shape=jax.ShapeDtypeStruct((chips, 2, half, width), BF16),
        cost_estimate=pl.CostEstimate(
            flops=4 * groups * group * half * held * width,
            bytes_accessed=2 * (2 * held * width + groups * group * half * width),
            transcendentals=0,
        ),
        name="pick_pieces",
    )(core, lists, near, mate)


def couple_kernel(first, last, *refs):
    refs = list(refs)
    weight_ref, occ_ref, energy_ref, arrived_hbm, margin_hbm, known_hbm, out_ref = refs[:7]
    refs = refs[7:]
    if not last:
        sent_ref, send_ref = refs[:2]
        refs = refs[2:]
    if first:
        margin_ref, refs = refs[0], refs[1:]
    other_ref, left_ref, held_ref, known_ref, sems = refs[:5]
    if first:
        turned_ref, basis_ref, arrived_ref = held_ref, refs[5], refs[6]
    else:
        margin_ref, arrived_ref = held_ref, arrived_hbm
    chips, _, steps, own, width = arrived_ref.shape
    orbitals = known_ref.shape[1]
    blocks = chips // TURN
    copies = []
    if first:
        for i in range(blocks):
            rows = pl.ds(i * TURN, TURN)
            copies.append(
                pltpu.make_async_copy(arrived_hbm.at[rows], arrived_ref.at[rows], sems.at[i])
            )
    margin_copy = pltpu.make_async_copy(margin_hbm, held_ref, sems.at[blocks])
    known_copy = pltpu.make_async_copy(known_hbm, known_ref, sems.at[blocks + 1])
    for copy in copies + [margin_copy, known_copy]:
        copy.start()
    order = regroup(TURN, own, False)
    for block in range(blocks):
        begin = block * TURN
        if first:
            copies[block].wait()
        for step in range(steps):
            for core in range(2):
                c = core * steps + step
                arrived = arrived_ref[begin : begin + TURN, core, step].reshape(TURN * own, width)
                moved = jnp.dot(order, arrived, preferred_element_type=F32).astype(BF16)
                for p in range(own):
                    rows = moved[p * TURN : (p + 1) * TURN]
                    for i in range(orbitals // chips):
                        place = i * chips + begin
                        other_ref[p, c, place : place + TURN, :] = part(rows, i)
                    for i in range(orbitals // chips, width // LANES):
                        place = i * chips + begin - orbitals
                        basis_ref[p, place : place + TURN, c * LANES : (c + 1) * LANES] = part(
                            rows, i
                        )
    margin_copy.wait()
    for p in range(own):
        if first:
            margin_ref[p] = jnp.dot(
                turned_ref[p], basis_ref[p], preferred_element_type=F32
            ).astype(BF16)
        for c in range(2 * steps):
            left = jnp.dot(
                margin_ref[p, :, c * orbitals : (c + 1) * orbitals],
                other_ref[p, c],
                preferred_element_type=F32,
            )
            left_ref[p, :, c * orbitals : (c + 1) * orbitals] = (left * weight_ref[p, c]).astype(
                BF16
            )
    known_copy.wait()
    stack = []
    for p in range(own):
        coupled = lax.dot_general(left_ref[p], margin_ref[p], NT, preferred_element_type=F32)
        energy = jnp.broadcast_to(energy_ref[p : p + 1, :], (orbitals, orbitals))
        divisor = energy.T + energy - occ_ref[p] + LEVEL_SHIFT
        amplitudes = known_ref[p] - coupled / divisor
        out_ref[p] = amplitudes
        if not last:
            sent = amplitudes.astype(BF16)
            sent_ref[p] = sent
            stack.append(sent)
    if not last:
        store_pieces(stack, send_ref, 0)


def couple(first, last, weights, occ, energy, arrived, margin, known):
    chips, _, steps, own, width = arrived.shape
    orbitals = known.shape[1]
    vectors = pl.BlockSpec(memory_space=pltpu.VMEM)
    far = pl.BlockSpec(memory_space=pltpu.HBM)
    scalars = pl.BlockSpec(memory_space=pltpu.SMEM)
    all_columns = 2 * steps * orbitals
    out_shape = [jax.ShapeDtypeStruct(known.shape, F32)]
    scratch_shapes = [
        pltpu.VMEM((own, 2 * steps, orbitals, orbitals), BF16),
        pltpu.VMEM((own, orbitals, all_columns), BF16),
        pltpu.VMEM(margin.shape, BF16),
        pltpu.VMEM(known.shape, F32),
        pltpu.SemaphoreType.DMA((chips // TURN + 2,)),
    ]
    if not last:
        out_shape += [
            jax.ShapeDtypeStruct(known.shape, BF16),
            jax.ShapeDtypeStruct((chips, own, orbitals // chips * LANES), BF16),
        ]
    if first:
        out_shape.append(jax.ShapeDtypeStruct((own, orbitals, all_columns), BF16))
        scratch_shapes.append(pltpu.VMEM((own, margin.shape[2], all_columns), BF16))
        scratch_shapes.append(pltpu.VMEM(arrived.shape, BF16))
    return pl.pallas_call(
        functools.partial(couple_kernel, first, last),
        in_specs=[scalars, scalars, vectors, far if first else vectors, far, far],
        out_specs=[vectors] * len(out_shape),
        out_shape=out_shape,
        scratch_shapes=scratch_shapes,
        compiler_params=None if first else pltpu.CompilerParams(vmem_limit_bytes=COUPLE_VMEM),
        name="couple",
    )(weights, occ, energy, arrived, margin, known)


def swap(values, groups=None):
    return lax.all_to_all(
        values, "pairs", split_axis=0, concat_axis=0, tiled=True, axis_index_groups=groups
    )


def shards(
    pno_basis,
    pno_count,
    partner_owner,
    partner_local,
    exchange_k,
    ladder_factor,
    pno_energy,
    occ_energy,
    coupling_fock,
):
    devices = lax.axis_size("pairs")
    chips = devices // 2
    own, domain, orbitals = pno_basis.shape
    fitted = ladder_factor.shape[1]
    partners = partner_owner.shape[1]
    half = own * partners // 2
    held = chips * own
    group = 32
    core = lax.rem(lax.axis_index("pairs"), 2).astype(jnp.int32)
    same_core = [list(range(k, devices, 2)) for k in range(2)]
    mates = [(i, i + 1 - 2 * (i % 2)) for i in range(devices)]
    columns = lax.broadcasted_iota(jnp.int32, (own, orbitals), 1)
    live_cols = (columns < pno_count[:, None]).astype(F32)
    energy_sum = pno_energy[:, :, None] + pno_energy[:, None, :] - occ_energy[:, None, None]
    divisor = energy_sum + LEVEL_SHIFT
    driving = exchange_k.astype(F32) * (live_cols[:, :, None] * live_cols[:, None, :])
    weights = coupling_fock.astype(F32)

    def ladder_of(sent):
        group_width = 8

        def add_group(group_index, total):
            factors = lax.dynamic_slice_in_dim(
                ladder_factor, group_index * group_width, group_width, 1
            )
            ladder_half = jnp.einsum(
                "rqac,rcd->rqad", factors, sent, preferred_element_type=F32
            ).astype(BF16)
            return total + jnp.einsum(
                "rqad,rqbd->rab", ladder_half, factors, preferred_element_type=F32
            )

        return lax.fori_loop(
            0, fitted // group_width, add_group, jnp.zeros((own, orbitals, orbitals), F32)
        )

    amplitudes, sent, margin, send = start(
        pno_count, occ_energy, partner_owner, partner_local, pno_basis, exchange_k, pno_energy, chips
    )
    lists = None
    for iteration in range(ITERS):
        first, last = iteration == 0, iteration == ITERS - 1
        near = swap(send, same_core)
        mate = lax.ppermute(near, "pairs", mates)
        width = 2 * LANES
        if first:
            width = near.shape[-1] - LANES
            names = slice(width, width + 2 * partners)
            asked = jnp.concatenate([near[:, :, names], mate[:, :, names]], axis=0)
            asked = asked.astype(jnp.int32).reshape(devices, own, 2, 2, partners // 2)
            asked = jnp.where(core == 0, asked[:, :, :, 0], asked[:, :, :, 1])
            owner, local = asked[:, :, 0], asked[:, :, 1]
            lists = jnp.bitwise_xor(owner % 2, core) * held + owner // 2 * own + local
            lists = lists.reshape(devices // group, group, own, partners // 2)
            lists = jnp.transpose(lists, (0, 3, 2, 1)).reshape(devices // group, half, group)
        tables = [table.reshape(held, table.shape[-1]) for table in (near, mate)]
        pieces = pick_pieces(core.reshape(1), lists, *tables, width)
        arrived = swap(pieces.reshape(devices, half, width))
        rest = driving + energy_sum * amplitudes + ladder_of(sent)
        known = amplitudes - rest / divisor
        results = couple(
            first,
            last,
            weights,
            occ_energy,
            pno_energy,
            arrived.reshape(chips, 2, partners // 2, own, width),
            margin,
            known,
        )
        amplitudes = results[0]
        if not last:
            sent, send = results[1], results[2]
        if first:
            margin = results[3]
    return amplitudes


def solution(mesh):
    return jax.shard_map(
        shards,
        mesh=mesh,
        in_specs=(
            P("pairs", None, None),
            P("pairs"),
            P("pairs", None),
            P("pairs", None),
            P("pairs", None, None),
            P("pairs", None, None, None),
            P("pairs", None),
            P("pairs"),
            P("pairs", None),
        ),
        out_specs=P("pairs", None, None),
        check_vma=False,
    )
```

```python
import functools

import jax
import jax.numpy as jnp
from jax import lax
from jax.experimental import pallas as pl
from jax.experimental.pallas import tpu as pltpu
from jax.sharding import PartitionSpec as P

ITERS = 3
LEVEL_SHIFT = 0.3
LANES = 128
TURN = 16
COUPLE_VMEM = 51 << 20
F32 = jnp.float32
BF16 = jnp.bfloat16
NT = (((1,), (1,)), ((), ()))


def regroup(major, minor):
    size = major * minor
    to = lax.broadcasted_iota(jnp.int32, (size, size), 0)
    source = lax.broadcasted_iota(jnp.int32, (size, size), 1)
    hit = source == lax.rem(to, minor) * major + lax.div(to, minor)
    return jnp.where(hit, 1.0, 0.0).astype(BF16)


def part(values, index):
    return values[:, index * LANES : (index + 1) * LANES]


def store_pieces(stack, send_ref, first_lane):
    chips, own, _ = send_ref.shape
    parts = stack[0].shape[0] // chips
    back = regroup(TURN, own)
    for start in range(0, chips, TURN):
        rows = jnp.concatenate(
            [
                jnp.concatenate(
                    [m[i * chips + start : i * chips + start + TURN] for i in range(parts)], axis=1
                )
                for m in stack
            ],
            axis=0,
        )
        pieces = jnp.dot(back, rows, preferred_element_type=F32).astype(BF16)
        pieces = pieces.reshape(TURN, own, parts * LANES)
        send_ref[start : start + TURN, :, first_lane : first_lane + parts * LANES] = pieces


def start_kernel(
    count_ref, occ_ref, owner_ref, local_ref, basis_ref, exchange_ref, energy_ref,
    amp_ref, sent_ref, turned_ref, send_ref,
):
    chips, own, width = send_ref.shape
    domain, orbitals = basis_ref.shape[1:]
    row = lax.broadcasted_iota(jnp.int32, (orbitals, orbitals), 0)
    col = lax.broadcasted_iota(jnp.int32, (orbitals, orbitals), 1)
    basis_col = lax.broadcasted_iota(jnp.int32, (domain, orbitals), 1)
    stack = []
    for p in range(own):
        count = count_ref[p]
        live = jnp.logical_and(row < count, col < count)
        energy = jnp.broadcast_to(energy_ref[p : p + 1, :], (orbitals, orbitals))
        energy_sum = energy.T + energy - occ_ref[p]
        driving = jnp.where(live, exchange_ref[p].astype(F32), 0.0)
        amplitudes = -driving / (energy_sum + LEVEL_SHIFT)
        amp_ref[p] = amplitudes
        sent = amplitudes.astype(BF16)
        sent_ref[p] = sent
        masked = jnp.where(basis_col < count, basis_ref[p].astype(F32), 0.0)
        turned_ref[p] = masked.T.astype(BF16)
        stack.append(jnp.concatenate([sent, masked.astype(BF16)], axis=0))
    store_pieces(stack, send_ref, 0)
    partners = owner_ref.shape[1]
    empty = jnp.zeros((own, LANES - 2 * partners), F32)
    asked = jnp.concatenate(
        [owner_ref[...].astype(F32), local_ref[...].astype(F32), empty], axis=1
    )
    send_ref[:, :, width - LANES :] = jnp.broadcast_to(
        asked.astype(BF16)[None], (chips, own, LANES)
    )


def start(count, occ, owner, local, basis, exchange, energy, chips):
    own, domain, orbitals = basis.shape
    width = ((orbitals + domain) // chips + 1) * LANES
    scalars, vectors = pl.BlockSpec(memory_space=pltpu.SMEM), pl.BlockSpec(memory_space=pltpu.VMEM)
    return pl.pallas_call(
        start_kernel,
        in_specs=[scalars] * 2 + [vectors] * 5,
        out_specs=[vectors] * 4,
        out_shape=[
            jax.ShapeDtypeStruct((own, orbitals, orbitals), F32),
            jax.ShapeDtypeStruct((own, orbitals, orbitals), BF16),
            jax.ShapeDtypeStruct((own, orbitals, domain), BF16),
            jax.ShapeDtypeStruct((chips, own, width), BF16),
        ],
        name="start",
    )(count, occ, owner, local, basis, exchange, energy)


def pick_kernel(core_ref, list_ref, near_ref, mate_ref, out_ref, onehot_ref):
    half, group = list_ref.shape[1:]
    held, width = near_ref.shape
    lane = lax.broadcasted_iota(jnp.int32, (half, LANES), 1).astype(F32).astype(BF16)
    one, zero = jnp.bfloat16(1), jnp.bfloat16(0)
    at_once = 4
    for begin in range(0, group, at_once):
        for member in range(begin, begin + at_once):
            wanted = jnp.broadcast_to(list_ref[0, :, member : member + 1], (half, LANES))
            tile_of = lax.shift_right_logical(wanted, 7).astype(F32).astype(BF16)
            lane_of = jnp.bitwise_and(wanted, LANES - 1).astype(F32).astype(BF16)
            hit = jnp.where(lane_of == lane, one, zero)
            for tile in range(2 * held // LANES):
                onehot_ref[
                    member * half : (member + 1) * half, tile * LANES : (tile + 1) * LANES
                ] = jnp.where(tile_of == jnp.bfloat16(tile), hit, zero)
        rows = slice(begin * half, (begin + at_once) * half)
        picked = jnp.dot(
            onehot_ref[rows, :held], near_ref[...], preferred_element_type=F32
        ) + jnp.dot(onehot_ref[rows, held:], mate_ref[...], preferred_element_type=F32)
        out_ref[begin : begin + at_once, 0] = picked.astype(BF16).reshape(at_once, half, width)


def pick_pieces(core, lists, near, mate, width):
    groups, half, group = lists.shape
    held = near.shape[0]
    chips = groups * group // 2
    halves = groups // 2
    table = pl.BlockSpec((held, width), lambda g, core: (0, 0))
    return pl.pallas_call(
        pick_kernel,
        grid_spec=pltpu.PrefetchScalarGridSpec(
            num_scalar_prefetch=1,
            grid=(groups,),
            in_specs=[pl.BlockSpec((1, half, group), lambda g, core: (g, 0, 0)), table, table],
            out_specs=pl.BlockSpec(
                (group, 1, half, width),
                lambda g, core: (
                    lax.rem(g, halves),
                    jnp.bitwise_xor(lax.div(g, halves), core[0]),
                    0,
                    0,
                ),
            ),
            scratch_shapes=[pltpu.VMEM((group * half, 2 * held), BF16)],
        ),
        out_shape=jax.ShapeDtypeStruct((chips, 2, half, width), BF16),
        cost_estimate=pl.CostEstimate(
            flops=4 * groups * group * half * held * width,
            bytes_accessed=2 * (2 * held * width + groups * group * half * width),
            transcendentals=0,
        ),
        name="pick_pieces",
    )(core, lists, near, mate)


def couple_kernel(first, last, *refs):
    refs = list(refs)
    weight_ref, occ_ref, energy_ref, arrived_hbm, margin_hbm, known_hbm, out_hbm = refs[:7]
    refs = refs[7:]
    if not last:
        sent_ref, send_ref = refs[:2]
        refs = refs[2:]
    if first:
        margin_ref, refs = refs[0], refs[1:]
    other_ref, left_ref, held_ref, known_ref, arrived_ref, sems = refs[:6]
    if first:
        turned_ref, basis_ref = held_ref, refs[6]
    else:
        margin_ref = held_ref
    chips, _, steps, own, width = arrived_ref.shape
    orbitals = known_ref.shape[1]
    blocks = chips // TURN
    copies = []
    for i in range(blocks):
        rows = pl.ds(i * TURN, TURN)
        copies.append(
            pltpu.make_async_copy(arrived_hbm.at[rows], arrived_ref.at[rows], sems.at[i])
        )
    margin_copy = pltpu.make_async_copy(margin_hbm, held_ref, sems.at[blocks])
    known_copy = pltpu.make_async_copy(known_hbm, known_ref, sems.at[blocks + 1])
    for copy in copies + [margin_copy, known_copy]:
        copy.start()
    for block in range(blocks):
        begin = block * TURN
        copies[block].wait()
        for step in range(steps):
            for core in range(2):
                c = core * steps + step
                arrived = arrived_ref[begin : begin + TURN, core, step]
                moved = jnp.transpose(arrived, (1, 0, 2))
                for p in range(own):
                    rows = moved[p]
                    for i in range(orbitals // chips):
                        place = i * chips + begin
                        other_ref[p, c, place : place + TURN, :] = part(rows, i)
                    for i in range(orbitals // chips, width // LANES):
                        place = i * chips + begin - orbitals
                        basis_ref[p, place : place + TURN, c * LANES : (c + 1) * LANES] = part(
                            rows, i
                        )
    margin_copy.wait()
    for p in range(own):
        if first:
            margin_ref[p] = jnp.dot(
                turned_ref[p], basis_ref[p], preferred_element_type=F32
            ).astype(BF16)
        for c in range(2 * steps):
            left = jnp.dot(
                margin_ref[p, :, c * orbitals : (c + 1) * orbitals],
                other_ref[p, c],
                preferred_element_type=F32,
            )
            left_ref[p, :, c * orbitals : (c + 1) * orbitals] = (left * weight_ref[p, c]).astype(
                BF16
            )
    known_copy.wait()
    stack, leaving = [], []
    for p in range(own):
        coupled = lax.dot_general(left_ref[p], margin_ref[p], NT, preferred_element_type=F32)
        energy = jnp.broadcast_to(energy_ref[p : p + 1, :], (orbitals, orbitals))
        divisor = energy.T + energy - occ_ref[p] + LEVEL_SHIFT
        amplitudes = known_ref[p] - coupled / divisor
        known_ref[p] = amplitudes
        leave = pltpu.make_async_copy(known_ref.at[p], out_hbm.at[p], sems.at[blocks + 2 + p])
        leave.start()
        leaving.append(leave)
        if not last:
            sent = amplitudes.astype(BF16)
            sent_ref[p] = sent
            stack.append(sent)
    if not last:
        store_pieces(stack, send_ref, 0)
    for leave in leaving:
        leave.wait()


def couple(first, last, weights, occ, energy, arrived, margin, known):
    chips, _, steps, own, width = arrived.shape
    orbitals = known.shape[1]
    vectors = pl.BlockSpec(memory_space=pltpu.VMEM)
    far = pl.BlockSpec(memory_space=pltpu.HBM)
    scalars = pl.BlockSpec(memory_space=pltpu.SMEM)
    all_columns = 2 * steps * orbitals
    out_shape = [jax.ShapeDtypeStruct(known.shape, F32)]
    scratch_shapes = [
        pltpu.VMEM((own, 2 * steps, orbitals, orbitals), BF16),
        pltpu.VMEM((own, orbitals, all_columns), BF16),
        pltpu.VMEM(margin.shape, BF16),
        pltpu.VMEM(known.shape, F32),
        pltpu.VMEM(arrived.shape, BF16),
        pltpu.SemaphoreType.DMA((chips // TURN + 2 + own,)),
    ]
    if not last:
        out_shape += [
            jax.ShapeDtypeStruct(known.shape, BF16),
            jax.ShapeDtypeStruct((chips, own, orbitals // chips * LANES), BF16),
        ]
    if first:
        out_shape.append(jax.ShapeDtypeStruct((own, orbitals, all_columns), BF16))
        scratch_shapes.append(pltpu.VMEM((own, margin.shape[2], all_columns), BF16))
    return pl.pallas_call(
        functools.partial(couple_kernel, first, last),
        in_specs=[scalars, scalars, vectors, far, far, far],
        out_specs=[far] + [vectors] * (len(out_shape) - 1),
        out_shape=out_shape,
        input_output_aliases={5: 0},
        scratch_shapes=scratch_shapes,
        compiler_params=None if first else pltpu.CompilerParams(vmem_limit_bytes=COUPLE_VMEM),
        name="couple",
    )(weights, occ, energy, arrived, margin, known)


def swap(values, groups=None):
    return lax.all_to_all(
        values, "pairs", split_axis=0, concat_axis=0, tiled=True, axis_index_groups=groups
    )


def shards(
    pno_basis,
    pno_count,
    partner_owner,
    partner_local,
    exchange_k,
    ladder_factor,
    pno_energy,
    occ_energy,
    coupling_fock,
):
    devices = lax.axis_size("pairs")
    chips = devices // 2
    own, domain, orbitals = pno_basis.shape
    fitted = ladder_factor.shape[1]
    partners = partner_owner.shape[1]
    half = own * partners // 2
    held = chips * own
    group = 32
    core = lax.rem(lax.axis_index("pairs"), 2).astype(jnp.int32)
    same_core = [list(range(k, devices, 2)) for k in range(2)]
    mates = [(i, i + 1 - 2 * (i % 2)) for i in range(devices)]
    columns = lax.broadcasted_iota(jnp.int32, (own, orbitals), 1)
    live_cols = (columns < pno_count[:, None]).astype(F32)
    energy_sum = pno_energy[:, :, None] + pno_energy[:, None, :] - occ_energy[:, None, None]
    divisor = energy_sum + LEVEL_SHIFT
    driving = exchange_k.astype(F32) * (live_cols[:, :, None] * live_cols[:, None, :])
    weights = coupling_fock.astype(F32)

    def ladder_of(sent):
        group_width = 8

        def add_group(group_index, total):
            factors = lax.dynamic_slice_in_dim(
                ladder_factor, group_index * group_width, group_width, 1
            )
            ladder_half = jnp.einsum(
                "rqac,rcd->rqad", factors, sent, preferred_element_type=F32
            ).astype(BF16)
            return total + jnp.einsum(
                "rqad,rqbd->rab", ladder_half, factors, preferred_element_type=F32
            )

        return lax.fori_loop(
            0, fitted // group_width, add_group, jnp.zeros((own, orbitals, orbitals), F32)
        )

    amplitudes, sent, margin, send = start(
        pno_count, occ_energy, partner_owner, partner_local, pno_basis, exchange_k, pno_energy, chips
    )
    lists = None
    for iteration in range(ITERS):
        first, last = iteration == 0, iteration == ITERS - 1
        near = swap(send, same_core)
        mate = lax.ppermute(near, "pairs", mates)
        width = 2 * LANES
        if first:
            width = near.shape[-1] - LANES
            names = slice(width, width + 2 * partners)
            asked = jnp.concatenate([near[:, :, names], mate[:, :, names]], axis=0)
            asked = asked.astype(jnp.int32).reshape(devices, own, 2, 2, partners // 2)
            asked = jnp.where(core == 0, asked[:, :, :, 0], asked[:, :, :, 1])
            owner, local = asked[:, :, 0], asked[:, :, 1]
            lists = jnp.bitwise_xor(owner % 2, core) * held + owner // 2 * own + local
            lists = lists.reshape(devices // group, group, own, partners // 2)
            lists = jnp.transpose(lists, (0, 3, 2, 1)).reshape(devices // group, half, group)
        tables = [table.reshape(held, table.shape[-1]) for table in (near, mate)]
        pieces = pick_pieces(core.reshape(1), lists, *tables, width)
        arrived = swap(pieces.reshape(devices, half, width))
        rest = driving + energy_sum * amplitudes + ladder_of(sent)
        known = amplitudes - rest / divisor
        results = couple(
            first,
            last,
            weights,
            occ_energy,
            pno_energy,
            arrived.reshape(chips, 2, partners // 2, own, width),
            margin,
            known,
        )
        amplitudes = results[0]
        if not last:
            sent, send = results[1], results[2]
        if first:
            margin = results[3]
    return amplitudes


def solution(mesh):
    return jax.shard_map(
        shards,
        mesh=mesh,
        in_specs=(
            P("pairs", None, None),
            P("pairs"),
            P("pairs", None),
            P("pairs", None),
            P("pairs", None, None),
            P("pairs", None, None, None),
            P("pairs", None),
            P("pairs"),
            P("pairs", None),
        ),
        out_specs=P("pairs", None, None),
        check_vma=False,
    )
```

```python
import functools

import jax
import jax.numpy as jnp
from jax import lax
from jax.experimental import pallas as pl
from jax.experimental.pallas import tpu as pltpu
from jax.sharding import PartitionSpec as P

ITERS = 3
LEVEL_SHIFT = 0.3
LANES = 128
TURN = 16
COUPLE_VMEM = 48 << 20
F32 = jnp.float32
BF16 = jnp.bfloat16
NT = (((1,), (1,)), ((), ()))


def regroup(major, minor):
    size = major * minor
    to = lax.broadcasted_iota(jnp.int32, (size, size), 0)
    source = lax.broadcasted_iota(jnp.int32, (size, size), 1)
    hit = source == lax.rem(to, minor) * major + lax.div(to, minor)
    return jnp.where(hit, 1.0, 0.0).astype(BF16)


def part(values, index):
    return values[:, index * LANES : (index + 1) * LANES]


def store_pieces(stack, send_ref, first_lane):
    chips, own, _ = send_ref.shape
    parts = stack[0].shape[0] // chips
    back = regroup(TURN, own)
    for start in range(0, chips, TURN):
        rows = jnp.concatenate(
            [
                jnp.concatenate(
                    [m[i * chips + start : i * chips + start + TURN] for i in range(parts)], axis=1
                )
                for m in stack
            ],
            axis=0,
        )
        pieces = jnp.dot(back, rows, preferred_element_type=F32).astype(BF16)
        pieces = pieces.reshape(TURN, own, parts * LANES)
        send_ref[start : start + TURN, :, first_lane : first_lane + parts * LANES] = pieces


def start_kernel(
    count_ref, occ_ref, owner_ref, local_ref, basis_ref, exchange_ref, energy_ref,
    amp_ref, sent_ref, turned_ref, send_ref,
):
    chips, own, width = send_ref.shape
    domain, orbitals = basis_ref.shape[1:]
    row = lax.broadcasted_iota(jnp.int32, (orbitals, orbitals), 0)
    col = lax.broadcasted_iota(jnp.int32, (orbitals, orbitals), 1)
    basis_col = lax.broadcasted_iota(jnp.int32, (domain, orbitals), 1)
    stack = []
    for p in range(own):
        count = count_ref[p]
        live = jnp.logical_and(row < count, col < count)
        energy = jnp.broadcast_to(energy_ref[p : p + 1, :], (orbitals, orbitals))
        energy_sum = energy.T + energy - occ_ref[p]
        driving = jnp.where(live, exchange_ref[p].astype(F32), 0.0)
        amplitudes = -driving / (energy_sum + LEVEL_SHIFT)
        amp_ref[p] = amplitudes
        sent = amplitudes.astype(BF16)
        sent_ref[p] = sent
        masked = jnp.where(basis_col < count, basis_ref[p].astype(F32), 0.0)
        turned_ref[p] = masked.T.astype(BF16)
        stack.append(jnp.concatenate([sent, masked.astype(BF16)], axis=0))
    store_pieces(stack, send_ref, 0)
    partners = owner_ref.shape[1]
    empty = jnp.zeros((own, LANES - 2 * partners), F32)
    asked = jnp.concatenate(
        [owner_ref[...].astype(F32), local_ref[...].astype(F32), empty], axis=1
    )
    send_ref[:, :, width - LANES :] = jnp.broadcast_to(
        asked.astype(BF16)[None], (chips, own, LANES)
    )


def start(count, occ, owner, local, basis, exchange, energy, chips):
    own, domain, orbitals = basis.shape
    width = ((orbitals + domain) // chips + 1) * LANES
    scalars, vectors = pl.BlockSpec(memory_space=pltpu.SMEM), pl.BlockSpec(memory_space=pltpu.VMEM)
    return pl.pallas_call(
        start_kernel,
        in_specs=[scalars] * 2 + [vectors] * 5,
        out_specs=[vectors] * 4,
        out_shape=[
            jax.ShapeDtypeStruct((own, orbitals, orbitals), F32),
            jax.ShapeDtypeStruct((own, orbitals, orbitals), BF16),
            jax.ShapeDtypeStruct((own, orbitals, domain), BF16),
            jax.ShapeDtypeStruct((chips, own, width), BF16),
        ],
        name="start",
    )(count, occ, owner, local, basis, exchange, energy)


def pick_kernel(core_ref, list_ref, near_ref, mate_ref, out_ref, onehot_ref):
    half, group = list_ref.shape[1:]
    held, width = near_ref.shape
    lane = lax.broadcasted_iota(jnp.int32, (half, LANES), 1).astype(F32).astype(BF16)
    one, zero = jnp.bfloat16(1), jnp.bfloat16(0)
    at_once = 4
    for begin in range(0, group, at_once):
        for member in range(begin, begin + at_once):
            wanted = jnp.broadcast_to(list_ref[0, :, member : member + 1], (half, LANES))
            tile_of = lax.shift_right_logical(wanted, 7).astype(F32).astype(BF16)
            lane_of = jnp.bitwise_and(wanted, LANES - 1).astype(F32).astype(BF16)
            hit = jnp.where(lane_of == lane, one, zero)
            for tile in range(2 * held // LANES):
                onehot_ref[
                    member * half : (member + 1) * half, tile * LANES : (tile + 1) * LANES
                ] = jnp.where(tile_of == jnp.bfloat16(tile), hit, zero)
        rows = slice(begin * half, (begin + at_once) * half)
        picked = jnp.dot(
            onehot_ref[rows, :held], near_ref[...], preferred_element_type=F32
        ) + jnp.dot(onehot_ref[rows, held:], mate_ref[...], preferred_element_type=F32)
        out_ref[begin : begin + at_once, 0] = picked.astype(BF16).reshape(at_once, half, width)


def pick_pieces(core, lists, near, mate, width):
    groups, half, group = lists.shape
    held = near.shape[0]
    chips = groups * group // 2
    halves = groups // 2
    table = pl.BlockSpec((held, width), lambda g, core: (0, 0))
    return pl.pallas_call(
        pick_kernel,
        grid_spec=pltpu.PrefetchScalarGridSpec(
            num_scalar_prefetch=1,
            grid=(groups,),
            in_specs=[pl.BlockSpec((1, half, group), lambda g, core: (g, 0, 0)), table, table],
            out_specs=pl.BlockSpec(
                (group, 1, half, width),
                lambda g, core: (
                    lax.rem(g, halves),
                    jnp.bitwise_xor(lax.div(g, halves), core[0]),
                    0,
                    0,
                ),
            ),
            scratch_shapes=[pltpu.VMEM((group * half, 2 * held), BF16)],
        ),
        out_shape=jax.ShapeDtypeStruct((chips, 2, half, width), BF16),
        cost_estimate=pl.CostEstimate(
            flops=4 * groups * group * half * held * width,
            bytes_accessed=2 * (2 * held * width + groups * group * half * width),
            transcendentals=0,
        ),
        name="pick_pieces",
    )(core, lists, near, mate)


def couple_kernel(first, last, *refs):
    refs = list(refs)
    weight_ref, occ_ref, energy_ref, arrived_hbm, margin_hbm, known_hbm, out_hbm = refs[:7]
    refs = refs[7:]
    if not last:
        sent_ref, send_ref = refs[:2]
        refs = refs[2:]
    if first:
        margin_ref, refs = refs[0], refs[1:]
    other_ref, left_ref, held_ref, known_ref, sems = refs[:5]
    if first:
        turned_ref, basis_ref, arrived_ref = held_ref, refs[5], refs[6]
    else:
        margin_ref, arrived_ref = held_ref, arrived_hbm
    chips, _, steps, own, width = arrived_ref.shape
    orbitals = known_ref.shape[1]
    blocks = chips // TURN
    copies = []
    if first:
        for i in range(blocks):
            rows = pl.ds(i * TURN, TURN)
            copies.append(
                pltpu.make_async_copy(arrived_hbm.at[rows], arrived_ref.at[rows], sems.at[i])
            )
    margin_copy = pltpu.make_async_copy(margin_hbm, held_ref, sems.at[blocks])
    known_copy = pltpu.make_async_copy(known_hbm, known_ref, sems.at[blocks + 1])
    for copy in copies + [margin_copy, known_copy]:
        copy.start()
    for block in range(blocks):
        begin = block * TURN
        if first:
            copies[block].wait()
        for step in range(steps):
            for core in range(2):
                c = core * steps + step
                arrived = arrived_ref[begin : begin + TURN, core, step]
                moved = jnp.transpose(arrived, (1, 0, 2))
                for p in range(own):
                    rows = moved[p]
                    for i in range(orbitals // chips):
                        place = i * chips + begin
                        other_ref[p, c, place : place + TURN, :] = part(rows, i)
                    for i in range(orbitals // chips, width // LANES):
                        place = i * chips + begin - orbitals
                        basis_ref[p, place : place + TURN, c * LANES : (c + 1) * LANES] = part(
                            rows, i
                        )
    margin_copy.wait()
    for p in range(own):
        if first:
            margin_ref[p] = jnp.dot(
                turned_ref[p], basis_ref[p], preferred_element_type=F32
            ).astype(BF16)
        for c in range(2 * steps):
            left = jnp.dot(
                margin_ref[p, :, c * orbitals : (c + 1) * orbitals],
                other_ref[p, c],
                preferred_element_type=F32,
            )
            left_ref[p, :, c * orbitals : (c + 1) * orbitals] = (left * weight_ref[p, c]).astype(
                BF16
            )
    known_copy.wait()
    stack, leaving = [], []
    for p in range(own):
        coupled = lax.dot_general(left_ref[p], margin_ref[p], NT, preferred_element_type=F32)
        energy = jnp.broadcast_to(energy_ref[p : p + 1, :], (orbitals, orbitals))
        divisor = energy.T + energy - occ_ref[p] + LEVEL_SHIFT
        amplitudes = known_ref[p] - coupled / divisor
        known_ref[p] = amplitudes
        leave = pltpu.make_async_copy(known_ref.at[p], out_hbm.at[p], sems.at[blocks + 2 + p])
        leave.start()
        leaving.append(leave)
        if not last:
            sent = amplitudes.astype(BF16)
            sent_ref[p] = sent
            stack.append(sent)
    if not last:
        store_pieces(stack, send_ref, 0)
    for leave in leaving:
        leave.wait()


def couple(first, last, weights, occ, energy, arrived, margin, known):
    chips, _, steps, own, width = arrived.shape
    orbitals = known.shape[1]
    vectors = pl.BlockSpec(memory_space=pltpu.VMEM)
    far = pl.BlockSpec(memory_space=pltpu.HBM)
    scalars = pl.BlockSpec(memory_space=pltpu.SMEM)
    all_columns = 2 * steps * orbitals
    out_shape = [jax.ShapeDtypeStruct(known.shape, F32)]
    scratch_shapes = [
        pltpu.VMEM((own, 2 * steps, orbitals, orbitals), BF16),
        pltpu.VMEM((own, orbitals, all_columns), BF16),
        pltpu.VMEM(margin.shape, BF16),
        pltpu.VMEM(known.shape, F32),
        pltpu.SemaphoreType.DMA((chips // TURN + 2 + own,)),
    ]
    if not last:
        out_shape += [
            jax.ShapeDtypeStruct(known.shape, BF16),
            jax.ShapeDtypeStruct((chips, own, orbitals // chips * LANES), BF16),
        ]
    if first:
        out_shape.append(jax.ShapeDtypeStruct((own, orbitals, all_columns), BF16))
        scratch_shapes.append(pltpu.VMEM((own, margin.shape[2], all_columns), BF16))
        scratch_shapes.append(pltpu.VMEM(arrived.shape, BF16))
    return pl.pallas_call(
        functools.partial(couple_kernel, first, last),
        in_specs=[scalars, scalars, vectors, far if first else vectors, far, far],
        out_specs=[far] + [vectors] * (len(out_shape) - 1),
        out_shape=out_shape,
        input_output_aliases={5: 0},
        scratch_shapes=scratch_shapes,
        compiler_params=None if first else pltpu.CompilerParams(vmem_limit_bytes=COUPLE_VMEM),
        name="couple",
    )(weights, occ, energy, arrived, margin, known)


def swap(values, groups=None):
    return lax.all_to_all(
        values, "pairs", split_axis=0, concat_axis=0, tiled=True, axis_index_groups=groups
    )


def shards(
    pno_basis,
    pno_count,
    partner_owner,
    partner_local,
    exchange_k,
    ladder_factor,
    pno_energy,
    occ_energy,
    coupling_fock,
):
    devices = lax.axis_size("pairs")
    chips = devices // 2
    own, domain, orbitals = pno_basis.shape
    fitted = ladder_factor.shape[1]
    partners = partner_owner.shape[1]
    half = own * partners // 2
    held = chips * own
    group = 32
    core = lax.rem(lax.axis_index("pairs"), 2).astype(jnp.int32)
    same_core = [list(range(k, devices, 2)) for k in range(2)]
    mates = [(i, i + 1 - 2 * (i % 2)) for i in range(devices)]
    columns = lax.broadcasted_iota(jnp.int32, (own, orbitals), 1)
    live_cols = (columns < pno_count[:, None]).astype(F32)
    energy_sum = pno_energy[:, :, None] + pno_energy[:, None, :] - occ_energy[:, None, None]
    divisor = energy_sum + LEVEL_SHIFT
    driving = exchange_k.astype(F32) * (live_cols[:, :, None] * live_cols[:, None, :])
    weights = coupling_fock.astype(F32)

    def ladder_of(sent):
        group_width = 8

        def add_group(group_index, total):
            factors = lax.dynamic_slice_in_dim(
                ladder_factor, group_index * group_width, group_width, 1
            )
            ladder_half = jnp.einsum(
                "rqac,rcd->rqad", factors, sent, preferred_element_type=F32
            ).astype(BF16)
            return total + jnp.einsum(
                "rqad,rqbd->rab", ladder_half, factors, preferred_element_type=F32
            )

        return lax.fori_loop(
            0, fitted // group_width, add_group, jnp.zeros((own, orbitals, orbitals), F32)
        )

    amplitudes, sent, margin, send = start(
        pno_count, occ_energy, partner_owner, partner_local, pno_basis, exchange_k, pno_energy, chips
    )
    lists = None
    for iteration in range(ITERS):
        first, last = iteration == 0, iteration == ITERS - 1
        near = swap(send, same_core)
        mate = lax.ppermute(near, "pairs", mates)
        width = 2 * LANES
        if first:
            width = near.shape[-1] - LANES
            names = slice(width, width + 2 * partners)
            asked = jnp.concatenate([near[:, :, names], mate[:, :, names]], axis=0)
            asked = asked.astype(jnp.int32).reshape(devices, own, 2, 2, partners // 2)
            asked = jnp.where(core == 0, asked[:, :, :, 0], asked[:, :, :, 1])
            owner, local = asked[:, :, 0], asked[:, :, 1]
            lists = jnp.bitwise_xor(owner % 2, core) * held + owner // 2 * own + local
            lists = lists.reshape(devices // group, group, own, partners // 2)
            lists = jnp.transpose(lists, (0, 3, 2, 1)).reshape(devices // group, half, group)
        tables = [table.reshape(held, table.shape[-1]) for table in (near, mate)]
        pieces = pick_pieces(core.reshape(1), lists, *tables, width)
        arrived = swap(pieces.reshape(devices, half, width))
        rest = driving + energy_sum * amplitudes + ladder_of(sent)
        known = amplitudes - rest / divisor
        results = couple(
            first,
            last,
            weights,
            occ_energy,
            pno_energy,
            arrived.reshape(chips, 2, partners // 2, own, width),
            margin,
            known,
        )
        amplitudes = results[0]
        if not last:
            sent, send = results[1], results[2]
        if first:
            margin = results[3]
    return amplitudes


def solution(mesh):
    return jax.shard_map(
        shards,
        mesh=mesh,
        in_specs=(
            P("pairs", None, None),
            P("pairs"),
            P("pairs", None),
            P("pairs", None),
            P("pairs", None, None),
            P("pairs", None, None, None),
            P("pairs", None),
            P("pairs"),
            P("pairs", None),
        ),
        out_specs=P("pairs", None, None),
        check_vma=False,
    )
```
